256 devices in a mesh: gx: 32 (over x, y, core), gy: 8 (over z).
Axes of the slice: x: 4, y: 4, z: 8, core: 2. Of those that a mesh axis runs over, the one named last changes fastest.
Arguments:
- tokens: bfloat16 [512, 16384], P('gy', 'gx'), may hold values from -6 to 6
- gate_weight: bfloat16 [16384, 26624], P('gx', 'gy'), may hold values from -0.046875 to 0.046875
- up_weight: bfloat16 [16384, 26624], P('gx', 'gy'), may hold values from -0.046875 to 0.046875
- down_weight: bfloat16 [26624, 16384], P('gy', 'gx'), may hold values from -0.0390625 to 0.0390625
Outputs:
- layer_out: bfloat16 [512, 16384], P('gy', 'gx')
The draws below stay inside these ranges and needn't reach their ends.
All inputs are finite; a program needn't handle non-finite values.
Results may differ from the reference program's by a relative error of at most 0.0049.
Values may be sent and summed in bfloat16 or wider, within the bound.
A program may use at most 128 MiB of HBM per device.

```python
import jax
import jax.numpy as jnp

D = 16384
HID = 26624
TOKENS = 512


def levels(stream_key, shape, split, low, largest):
    loudness = 1.0
    for position, parts in split:
        steps = jax.random.uniform(jax.random.fold_in(jax.random.fold_in(stream_key, 6), position), (parts,), jnp.float32, low / len(split), largest / len(split))
        loudness = loudness * jnp.repeat(jnp.exp(steps), shape[position] // parts).reshape((-1,) + (1,) * (len(shape) - 1 - position))
    return loudness


def scatter_about(key, dims, scale, most, pieces=(), dtype=jnp.bfloat16):
    values = jax.random.normal(key, dims, jnp.float32) * scale
    if len(pieces) > 0:
        values = levels(key, dims, pieces, -0.22, 0.18) * values
    return jnp.clip(values, min=-most, max=most).astype(dtype)


def setup_inputs(seed: int = 0) -> dict:
    key_of = jax.random.split(jax.random.key(seed), 5)
    return {
        "tokens": scatter_about(key_of[0], (TOKENS, D), 1.0, 6.0, ((0, 8), (1, 32))),
        "gate_weight": scatter_about(key_of[1], (D, HID), D ** -0.5, 0.046875, ((0, 32), (1, 8))),
        "up_weight": scatter_about(key_of[2], (D, HID), D ** -0.5, 0.046875, ((0, 32), (1, 8))),
        "down_weight": scatter_about(key_of[3], (HID, D), HID ** -0.5, 0.0390625, ((0, 8), (1, 32))),
    }


def reference(tokens, gate_weight, up_weight, down_weight):
    gate = jnp.dot(tokens, gate_weight, preferred_element_type=jnp.float32)
    up = jnp.dot(tokens, up_weight, preferred_element_type=jnp.float32)
    hidden = (jax.nn.silu(gate) * up).astype(jnp.bfloat16)
    return jnp.dot(hidden, down_weight, preferred_element_type=jnp.float32).astype(jnp.bfloat16)
```

```python
import functools

import jax
import jax.numpy as jnp
from jax import lax
from jax.experimental import pallas as pl
from jax.experimental.pallas import tpu as pltpu
from jax.sharding import PartitionSpec as P

MESH = pl.DeviceIdType.MESH
GROUPS = 4
PIECES = (896, 768)
OWNERS = ((0, 7), (2, 5), (4, 3), (1, 6))
TILE = 256
LAGS = (0, 2, 4, 6, 8, 9)


def kernel(tok_hbm, gate_hbm, up_hbm, down_hbm, out_ref,
           wb, wd, tokc, pf, pb, r1, s2f, s2b, r2, hid, yf, yb, zr,
           loc_sem, w_ss, w_rs, t_ss, t_rs, f_ss, f_rs, s1_ss, s1_rs, s2_ss, s2_rs,
           g1_ss, g1_rs, g2_ss, g2_rs, sib_ss, sib_rs, z_ss, z_rs):
    gx = lax.axis_index("gx")
    z = lax.axis_index("gy")
    core = gx % 2
    y = (gx // 2) % 4
    x = gx // 8
    half = wb.shape[2] // 2
    cols = wb.shape[2]
    p = x * (1 - core) + y * core
    q = y * (1 - core) + x * core

    def device(x_, y_, core_, z_):
        return {"gx": (x_ % 4) * 8 + (y_ % 4) * 2 + core_, "gy": z_ % 8}

    def first(step):
        return device(x + step * (1 - core), y + step * core, core, z)

    def second(step):
        return device(x + step * core, y + step * (1 - core), core, z)

    def along_z(step):
        return device(x, y, core, z + step)

    sibling = device(x, y, 1 - core, z)

    def remote(src, dst, ss, rs, to):
        return pltpu.make_async_remote_copy(src_ref=src, dst_ref=dst, send_sem=ss, recv_sem=rs, device_id=to, device_id_type=MESH)

    sent = []

    def go(copy):
        copy.start()
        sent.append(copy)
        return copy

    rows = tok_hbm.shape[0]
    starts = [sum(PIECES[:h]) for h in range(len(PIECES))]
    slot = {o: (g, j) for g in range(GROUPS) for j, o in enumerate(OWNERS[g])}

    def tokens_at(o):
        g, j = slot[o]
        return tokc.at[g, core, pl.ds(j * rows, rows)]

    def weight_copies(owner, h, make):
        copies = []
        for i, hbm in enumerate((gate_hbm, up_hbm)):
            src = hbm.at[:, pl.ds(pl.multiple_of(owner * half + starts[h], 128), PIECES[h])]
            dst = wb.at[core, :, pl.ds(2 * starts[h] + i * PIECES[h], PIECES[h])]
            copies.append(make(src, dst, 2 * h + i))
        return copies

    own_tokens = pltpu.make_async_copy(tok_hbm, tokens_at(0), loc_sem.at[0])
    own_tokens.start()
    own_weights = [weight_copies(core, h, lambda src, dst, i: pltpu.make_async_copy(src, dst, loc_sem.at[2 + i])) for h in range(2)]
    own_down = pltpu.make_async_copy(down_hbm, wd, loc_sem.at[1])
    for copy in own_weights[0]:
        copy.start()

    barrier = pltpu.get_barrier_semaphore()
    peers = [sibling, first(1), first(2), first(3), second(1), second(2), second(3)] + [along_z(s) for s in range(1, 8)]
    for peer in peers:
        pl.semaphore_signal(barrier, inc=1, device_id=peer, device_id_type=MESH)
    pl.semaphore_wait(barrier, len(peers))

    def swap_weights(h):
        return weight_copies(1 - core, h, lambda src, dst, i: go(remote(src, dst, w_ss.at[i], w_rs.at[i], sibling)))

    def pass_tokens(src, o, step):
        return go(remote(src, tokens_at(o), t_ss.at[o], t_rs.at[o], along_z(step)))

    def share_tokens(o):
        return go(remote(tokens_at(o), tokens_at(o), f_ss.at[o], f_rs.at[o], sibling))

    arrive = {1: pass_tokens(tok_hbm, 1, 7), 7: pass_tokens(tok_hbm, 7, 1)}
    swapped = [swap_weights(0)]
    for h in range(1, len(PIECES)):
        for copy in own_weights[h]:
            copy.start()
    own_down.start()
    own_tokens.wait()
    shared = {0: share_tokens(0)}

    def relay(distance):
        for o in (distance, 8 - distance)[:1 if distance == 4 else 2]:
            arrive[o].wait_recv()
            shared[o] = share_tokens(o)
            if o < 4:
                arrive[o + 1] = pass_tokens(tokens_at(o), o + 1, 7)
            elif o > 5:
                arrive[o - 1] = pass_tokens(tokens_at(o), o - 1, 1)

    def weights_ready(h):
        for copy in own_weights[h]:
            copy.wait()
        for copy in swapped[h]:
            copy.wait_recv()

    def span(h, width=2):
        return pl.ds(width * starts[h], width * PIECES[h])

    def over_tiles(h, body):
        @pl.loop(0, 2 * PIECES[h] // TILE)
        def _(n):
            body(pl.ds(pl.multiple_of(2 * starts[h] + n * TILE, TILE), TILE))

    s1, s2, g1, g2, sib = {}, {}, {}, {}, {}
    zs = {}

    def scatter(c, src, dst, ss, rs, to):
        i = 2 * c[0] + c[1]
        return [go(remote(src(d), dst(d), ss.at[i, d - 1], rs.at[i, d - 1], to(d))) for d in (2, 1, 3)]

    def stage_m(c):
        g, h = c
        if h == 0:
            for o in OWNERS[g]:
                shared[o].wait_recv()

        def body(at):
            acc = jnp.dot(tokc[g, 0], wb[0, :, at], preferred_element_type=jnp.float32)
            acc += jnp.dot(tokc[g, 1], wb[1, :, at], preferred_element_type=jnp.float32)
            pf[g, :, :, at] = acc.reshape(4, 32, TILE)
            pb[g, :, :, at] = acc.astype(jnp.bfloat16).reshape(4, 32, TILE)

        over_tiles(h, body)
        s1[c] = scatter(c, lambda d: pb.at[g, (p + d) % 4, :, span(h)], lambda d: r1.at[g, d - 1, :, span(h)], s1_ss, s1_rs, first)

    def stage_1(c):
        g, h = c
        for copy in s1[c]:
            copy.wait_recv()

        def body(at):
            acc = pf[g, p, :, at]
            for d in range(3):
                acc += r1[g, d, :, at].astype(jnp.float32)
            acc = acc.reshape(4, 8, TILE)
            s2f[g, :, :, at] = acc
            s2b[g, :, :, at] = acc.astype(jnp.bfloat16)

        over_tiles(h, body)
        s2[c] = scatter(c, lambda d: s2b.at[g, (q + d) % 4, :, span(h)], lambda d: r2.at[g, d - 1, :, span(h)], s2_ss, s2_rs, second)

    def stage_2(c):
        g, h = c
        for copy in s2[c]:
            copy.wait_recv()
        acc = s2f[g, q, :, span(h)]
        for d in range(3):
            acc += r2[g, d, :, span(h)].astype(jnp.float32)
        gate, up = acc[:, :PIECES[h]], acc[:, PIECES[h]:]
        hid[core, g, p * 4 + q, :, span(h, 1)] = (gate / (1.0 + jnp.exp(-gate)) * up).astype(jnp.bfloat16)
        place = hid.at[core, g, p * 4 + q, :, span(h, 1)]
        g1[c] = scatter(c, lambda d: place, lambda d: place, g1_ss, g1_rs, second)

    def stage_3(c):
        g, h = c
        for copy in g1[c]:
            copy.wait_recv()
        place = hid.at[core, g, pl.ds(p * 4, 4), :, span(h, 1)]
        g2[c] = scatter(c, lambda d: place, lambda d: place, g2_ss, g2_rs, first)

    def stage_4(c):
        g, h = c
        for copy in g2[c]:
            copy.wait_recv()
        place = hid.at[core, g, :, :, span(h, 1)]
        sib[c] = go(remote(place, place, sib_ss.at[2 * g + h], sib_rs.at[2 * g + h], sibling))

    def stage_5(c):
        g, h = c
        if h != len(PIECES) - 1:
            return
        for h in range(len(PIECES)):
            sib[g, h].wait_recv()
        if g == 0:
            own_down.wait()
        acc = None
        for i in range(2):
            units = hid[i, g].astype(jnp.float32).reshape(128, half).astype(jnp.bfloat16)
            term = jnp.dot(units, wd[pl.ds(i * half, half), :], preferred_element_type=jnp.float32)
            acc = term if acc is None else acc + term
        for j in range(2):
            o = OWNERS[g][j]
            part = acc[j * rows:(j + 1) * rows]
            if o == 0:
                yf[...] = part
            else:
                yb[o] = part.astype(jnp.bfloat16)
                zs[o] = go(remote(yb.at[o], zr.at[o], z_ss.at[o], z_rs.at[o], along_z(o)))

    chunks = [(g, h) for g in range(GROUPS) for h in range(len(PIECES))]
    stages = (stage_m, stage_1, stage_2, stage_3, stage_4, stage_5)
    relay(1)
    weights_ready(0)
    swapped.append(swap_weights(1))
    for t in range(len(chunks) + LAGS[-1]):
        for stage, lag in zip(stages, LAGS):
            if 0 <= t - lag < len(chunks):
                stage(chunks[t - lag])
        if t < 3:
            relay(t + 2)
        if t == 0:
            weights_ready(1)

    total = yf[...]
    for g in range(GROUPS):
        for o in OWNERS[g]:
            if o:
                zs[o].wait_recv()
                total += zr[o].astype(jnp.float32)
    out_ref[...] = total.astype(jnp.bfloat16)
    for copy in sent:
        copy.wait_send()


def on_device(tokens, gate_weight, up_weight, down_weight):
    rows, depth = tokens.shape
    hidden = gate_weight.shape[1]
    half = hidden // 2
    bf16, f32 = jnp.bfloat16, jnp.float32
    dma = pltpu.SemaphoreType.DMA
    n = GROUPS
    m = 2 * n
    return pl.pallas_call(
        kernel,
        out_shape=jax.ShapeDtypeStruct((rows, down_weight.shape[1]), bf16),
        in_specs=[pl.BlockSpec(memory_space=pl.ANY)] * 4,
        out_specs=pl.BlockSpec(memory_space=pltpu.VMEM),
        scratch_shapes=[
            pltpu.VMEM((2, depth, hidden), bf16),
            pltpu.VMEM(down_weight.shape, bf16),
            pltpu.VMEM((n, 2, 2 * rows, depth), bf16),
            pltpu.VMEM((n, 4, 32, hidden), f32),
            pltpu.VMEM((n, 4, 32, hidden), bf16),
            pltpu.VMEM((n, 3, 32, hidden), bf16),
            pltpu.VMEM((n, 4, 8, hidden), f32),
            pltpu.VMEM((n, 4, 8, hidden), bf16),
            pltpu.VMEM((n, 3, 8, hidden), bf16),
            pltpu.VMEM((2, n, 16, 8, half), bf16),
            pltpu.VMEM((rows, down_weight.shape[1]), f32),
            pltpu.VMEM((8, rows, down_weight.shape[1]), bf16),
            pltpu.VMEM((8, rows, down_weight.shape[1]), bf16),
            dma((6,)), dma((4,)), dma((4,)),
            dma((8,)), dma((8,)), dma((8,)), dma((8,)),
            dma((m, 3)), dma((m, 3)), dma((m, 3)), dma((m, 3)),
            dma((m, 3)), dma((m, 3)), dma((m, 3)), dma((m, 3)),
            dma((m,)), dma((m,)), dma((8,)), dma((8,)),
        ],
        compiler_params=pltpu.CompilerParams(collective_id=0, has_side_effects=True, vmem_limit_bytes=56 << 20),
    )(tokens, gate_weight, up_weight, down_weight)


def solution(mesh):
    return jax.shard_map(
        on_device,
        mesh=mesh,
        in_specs=(P("gy", "gx"), P("gx", "gy"), P("gx", "gy"), P("gy", "gx")),
        out_specs=P("gy", "gx"),
        check_vma=False,
    )
```

```python
import functools

import jax
import jax.numpy as jnp
from jax import lax
from jax.experimental import pallas as pl
from jax.experimental.pallas import tpu as pltpu
from jax.sharding import PartitionSpec as P

MESH = pl.DeviceIdType.MESH
GROUPS = 4
PIECES = (896, 768)
OWNERS = ((0, 7), (2, 5), (4, 3), (6, 1))
TILE = 256
LAGS = (0, 2, 4, 6, 8, 9)
RELAYS = {0: 2, 1: 3, 3: 4}


def kernel(tok_hbm, gate_hbm, up_hbm, down_hbm, out_ref,
           wb, wd, tokc, pf, pb, r1, s2f, s2b, r2, hid, ya, yb, zr,
           loc_sem, w_ss, w_rs, t_ss, t_rs, f_ss, f_rs, s1_ss, s1_rs, s2_ss, s2_rs,
           g1_ss, g1_rs, g2_ss, g2_rs, sib_ss, sib_rs, z_ss, z_rs):
    gx = lax.axis_index("gx")
    z = lax.axis_index("gy")
    core = gx % 2
    y = (gx // 2) % 4
    x = gx // 8
    half = wb.shape[2] // 2
    cols = wb.shape[2]
    p = x * (1 - core) + y * core
    q = y * (1 - core) + x * core

    def device(x_, y_, core_, z_):
        return {"gx": (x_ % 4) * 8 + (y_ % 4) * 2 + core_, "gy": z_ % 8}

    def first(step):
        return device(x + step * (1 - core), y + step * core, core, z)

    def second(step):
        return device(x + step * core, y + step * (1 - core), core, z)

    def along_z(step):
        return device(x, y, core, z + step)

    sibling = device(x, y, 1 - core, z)

    def remote(src, dst, ss, rs, to):
        return pltpu.make_async_remote_copy(src_ref=src, dst_ref=dst, send_sem=ss, recv_sem=rs, device_id=to, device_id_type=MESH)

    sent = []

    def go(copy):
        copy.start()
        sent.append(copy)
        return copy

    rows = tok_hbm.shape[0]
    starts = [sum(PIECES[:h]) for h in range(len(PIECES))]
    slot = {o: (g, j) for g in range(GROUPS) for j, o in enumerate(OWNERS[g])}

    def tokens_at(o):
        g, j = slot[o]
        return tokc.at[g, core, pl.ds(j * rows, rows)]

    def weight_copies(owner, h, make):
        copies = []
        for i, hbm in enumerate((gate_hbm, up_hbm)):
            src = hbm.at[:, pl.ds(pl.multiple_of(owner * half + starts[h], 128), PIECES[h])]
            dst = wb.at[core, :, pl.ds(2 * starts[h] + i * PIECES[h], PIECES[h])]
            copies.append(make(src, dst, 2 * h + i))
        return copies

    own_tokens = pltpu.make_async_copy(tok_hbm, tokens_at(0), loc_sem.at[0])
    own_tokens.start()
    own_weights = [weight_copies(core, h, lambda src, dst, i: pltpu.make_async_copy(src, dst, loc_sem.at[2 + i])) for h in range(2)]
    own_down = pltpu.make_async_copy(down_hbm, wd, loc_sem.at[1])
    for copy in own_weights[0]:
        copy.start()

    barrier = pltpu.get_barrier_semaphore()
    peers = [sibling, first(1), first(2), first(3), second(1), second(2), second(3)] + [along_z(s) for s in (1, 7)]
    for peer in peers:
        pl.semaphore_signal(barrier, inc=1, device_id=peer, device_id_type=MESH)
    pl.semaphore_wait(barrier, len(peers))

    def swap_weights(h):
        return weight_copies(1 - core, h, lambda src, dst, i: go(remote(src, dst, w_ss.at[i], w_rs.at[i], sibling)))

    def pass_tokens(src, o, step):
        return go(remote(src, tokens_at(o), t_ss.at[o], t_rs.at[o], along_z(step)))

    def share_tokens(o):
        return go(remote(tokens_at(o), tokens_at(o), f_ss.at[o], f_rs.at[o], sibling))

    arrive = {1: pass_tokens(tok_hbm, 1, 7), 7: pass_tokens(tok_hbm, 7, 1)}
    swapped = [swap_weights(0)]
    for h in range(1, len(PIECES)):
        for copy in own_weights[h]:
            copy.start()
    own_down.start()
    own_tokens.wait()
    shared = {0: share_tokens(0)}

    def relay(distance):
        for o in (distance, 8 - distance)[:1 if distance == 4 else 2]:
            arrive[o].wait_recv()
            shared[o] = share_tokens(o)
            if o < 4:
                arrive[o + 1] = pass_tokens(tokens_at(o), o + 1, 7)
            elif o > 5:
                arrive[o - 1] = pass_tokens(tokens_at(o), o - 1, 1)

    def weights_ready(h):
        for copy in own_weights[h]:
            copy.wait()
        for copy in swapped[h]:
            copy.wait_recv()

    def span(h, width=2):
        return pl.ds(width * starts[h], width * PIECES[h])

    def over_tiles(h, body):
        @pl.loop(0, 2 * PIECES[h] // TILE)
        def _(n):
            body(pl.ds(pl.multiple_of(2 * starts[h] + n * TILE, TILE), TILE))

    s1, s2, g1, g2, sib = {}, {}, {}, {}, {}
    zs = {}

    def scatter(c, src, dst, landing, ss, rs, to):
        i = 2 * c[0] + c[1]
        for d in (2, 1, 3):
            remote(src(d), dst(d), ss.at[i], rs.at[i], to(d)).start()
        three = remote(landing, landing, ss.at[i], rs.at[i], to(1))
        sent.append(three)
        return three

    def stage_m(c):
        g, h = c
        if h == 0:
            for o in OWNERS[g]:
                shared[o].wait_recv()

        def body(at):
            acc = jnp.dot(tokc[g, 0], wb[0, :, at], preferred_element_type=jnp.float32)
            acc += jnp.dot(tokc[g, 1], wb[1, :, at], preferred_element_type=jnp.float32)
            pf[g, :, :, at] = acc.reshape(4, 32, TILE)
            pb[g, :, :, at] = acc.astype(jnp.bfloat16).reshape(4, 32, TILE)

        over_tiles(h, body)
        s1[c] = scatter(c, lambda d: pb.at[g, (p + d) % 4, :, span(h)], lambda d: r1.at[g, d - 1, :, span(h)], r1.at[g, :, :, span(h)], s1_ss, s1_rs, first)

    def stage_1(c):
        g, h = c
        s1[c].wait_recv()

        def body(at):
            acc = pf[g, p, :, at]
            for d in range(3):
                acc += r1[g, d, :, at].astype(jnp.float32)
            acc = acc.reshape(4, 8, TILE)
            s2f[g, :, :, at] = acc
            s2b[g, :, :, at] = acc.astype(jnp.bfloat16)

        over_tiles(h, body)
        s2[c] = scatter(c, lambda d: s2b.at[g, (q + d) % 4, :, span(h)], lambda d: r2.at[g, d - 1, :, span(h)], r2.at[g, :, :, span(h)], s2_ss, s2_rs, second)

    def stage_2(c):
        g, h = c
        s2[c].wait_recv()
        acc = s2f[g, q, :, span(h)]
        for d in range(3):
            acc += r2[g, d, :, span(h)].astype(jnp.float32)
        gate, up = acc[:, :PIECES[h]], acc[:, PIECES[h]:]
        hid[core, g, p * 4 + q, :, span(h, 1)] = (gate / (1.0 + jnp.exp(-gate)) * up).astype(jnp.bfloat16)
        place = hid.at[core, g, p * 4 + q, :, span(h, 1)]
        g1[c] = scatter(c, lambda d: place, lambda d: place, hid.at[core, g, pl.ds(0, 3), :, span(h, 1)], g1_ss, g1_rs, second)

    def stage_3(c):
        g, h = c
        g1[c].wait_recv()
        place = hid.at[core, g, pl.ds(p * 4, 4), :, span(h, 1)]
        g2[c] = scatter(c, lambda d: place, lambda d: place, hid.at[core, g, pl.ds(0, 12), :, span(h, 1)], g2_ss, g2_rs, first)

    def stage_4(c):
        g, h = c
        g2[c].wait_recv()
        place = hid.at[core, g, :, :, span(h, 1)]
        sib[c] = go(remote(place, place, sib_ss.at[2 * g + h], sib_rs.at[2 * g + h], sibling))

    def stage_5(c):
        g, h = c
        sib[c].wait_recv()
        if c == (0, 0):
            own_down.wait()
        last = h == len(PIECES) - 1
        for j in range(2):
            o = OWNERS[g][j]
            part = None if h == 0 else ya[g, j]
            for i in range(2):
                units = hid[i, g, pl.ds(8 * j, 8), :, span(h, 1)].astype(jnp.float32).reshape(rows, PIECES[h]).astype(jnp.bfloat16)
                term = jnp.dot(units, wd[pl.ds(i * half + starts[h], PIECES[h]), :], preferred_element_type=jnp.float32)
                part = term if part is None else part + term
            if not last or o == 0:
                ya[g, j] = part
            else:
                yb[o] = part.astype(jnp.bfloat16)
                zs[o] = go(remote(yb.at[o], zr.at[o], z_ss.at[o], z_rs.at[o], along_z(o)))

    chunks = [(g, h) for g in range(GROUPS) for h in range(len(PIECES))]
    stages = (stage_m, stage_1, stage_2, stage_3, stage_4, stage_5)
    relay(1)
    weights_ready(0)
    swapped.append(swap_weights(1))
    for t in range(len(chunks) + LAGS[-1]):
        for stage, lag in zip(stages, LAGS):
            if 0 <= t - lag < len(chunks):
                stage(chunks[t - lag])
        if t in RELAYS:
            relay(RELAYS[t])
        if t == 0:
            weights_ready(1)

    for copy in sent:
        copy.wait_send()
    total = ya[0, 0]
    for g in range(GROUPS):
        for o in OWNERS[g]:
            if o:
                zs[o].wait_recv()
                total += zr[o].astype(jnp.float32)
    out_ref[...] = total.astype(jnp.bfloat16)


def on_device(tokens, gate_weight, up_weight, down_weight):
    rows, depth = tokens.shape
    hidden = gate_weight.shape[1]
    half = hidden // 2
    bf16, f32 = jnp.bfloat16, jnp.float32
    dma = pltpu.SemaphoreType.DMA
    n = GROUPS
    m = 2 * n
    return pl.pallas_call(
        kernel,
        out_shape=jax.ShapeDtypeStruct((rows, down_weight.shape[1]), bf16),
        in_specs=[pl.BlockSpec(memory_space=pl.ANY)] * 4,
        out_specs=pl.BlockSpec(memory_space=pltpu.VMEM),
        scratch_shapes=[
            pltpu.VMEM((2, depth, hidden), bf16),
            pltpu.VMEM(down_weight.shape, bf16),
            pltpu.VMEM((n, 2, 2 * rows, depth), bf16),
            pltpu.VMEM((n, 4, 32, hidden), f32),
            pltpu.VMEM((n, 4, 32, hidden), bf16),
            pltpu.VMEM((n, 3, 32, hidden), bf16),
            pltpu.VMEM((n, 4, 8, hidden), f32),
            pltpu.VMEM((n, 4, 8, hidden), bf16),
            pltpu.VMEM((n, 3, 8, hidden), bf16),
            pltpu.VMEM((2, n, 16, 8, half), bf16),
            pltpu.VMEM((n, 2, rows, down_weight.shape[1]), f32),
            pltpu.VMEM((8, rows, down_weight.shape[1]), bf16),
            pltpu.VMEM((8, rows, down_weight.shape[1]), bf16),
            dma((6,)), dma((4,)), dma((4,)),
            dma((8,)), dma((8,)), dma((8,)), dma((8,)),
            dma((m,)), dma((m,)), dma((m,)), dma((m,)),
            dma((m,)), dma((m,)), dma((m,)), dma((m,)),
            dma((m,)), dma((m,)), dma((8,)), dma((8,)),
        ],
        compiler_params=pltpu.CompilerParams(collective_id=0, has_side_effects=True, vmem_limit_bytes=56 << 20),
    )(tokens, gate_weight, up_weight, down_weight)


def solution(mesh):
    return jax.shard_map(
        on_device,
        mesh=mesh,
        in_specs=(P("gy", "gx"), P("gx", "gy"), P("gx", "gy"), P("gy", "gx")),
        out_specs=P("gy", "gx"),
        check_vma=False,
    )
```

```python
import functools

import jax
import jax.numpy as jnp
from jax import lax
from jax.experimental import pallas as pl
from jax.experimental.pallas import tpu as pltpu
from jax.sharding import PartitionSpec as P

MESH = pl.DeviceIdType.MESH
GROUPS = 4
PIECES = (896, 768)
OWNERS = ((0, 7), (2, 5), (4, 3), (6, 1))
TILE = 256
LAGS = (0, 2, 4, 6, 8, 9)
RELAYS = {0: 2, 1: 3, 3: 4}


def kernel(tok_hbm, gate_hbm, up_hbm, down_hbm, out_ref,
           wb, wd, tokc, pf, pb, r1, s2f, s2b, r2, hid, ya, yb, zr,
           loc_sem, w_ss, w_rs, t_ss, t_rs, f_ss, f_rs, s1_ss, s1_rs, s2_ss, s2_rs,
           g1_ss, g1_rs, g2_ss, g2_rs, sib_ss, sib_rs, z_ss, z_rs):
    gx = lax.axis_index("gx")
    z = lax.axis_index("gy")
    core = gx % 2
    y = (gx // 2) % 4
    x = gx // 8
    half = wb.shape[2] // 2
    cols = wb.shape[2]
    p = x * (1 - core) + y * core
    q = y * (1 - core) + x * core

    def device(x_, y_, core_, z_):
        return {"gx": (x_ % 4) * 8 + (y_ % 4) * 2 + core_, "gy": z_ % 8}

    def first(step):
        return device(x + step * (1 - core), y + step * core, core, z)

    def second(step):
        return device(x + step * core, y + step * (1 - core), core, z)

    def along_z(step):
        return device(x, y, core, z + step)

    sibling = device(x, y, 1 - core, z)

    def remote(src, dst, ss, rs, to):
        return pltpu.make_async_remote_copy(src_ref=src, dst_ref=dst, send_sem=ss, recv_sem=rs, device_id=to, device_id_type=MESH)

    sent = []

    def go(copy):
        copy.start()
        sent.append(copy)
        return copy

    rows = tok_hbm.shape[0]
    starts = [sum(PIECES[:h]) for h in range(len(PIECES))]
    slot = {o: (g, j) for g in range(GROUPS) for j, o in enumerate(OWNERS[g])}

    def tokens_at(o):
        g, j = slot[o]
        return tokc.at[g, core, pl.ds(j * rows, rows)]

    def weight_copies(owner, h, make):
        copies = []
        for i, hbm in enumerate((gate_hbm, up_hbm)):
            src = hbm.at[:, pl.ds(pl.multiple_of(owner * half + starts[h], 128), PIECES[h])]
            dst = wb.at[core, :, pl.ds(2 * starts[h] + i * PIECES[h], PIECES[h])]
            copies.append(make(src, dst, 2 * h + i))
        return copies

    own_tokens = pltpu.make_async_copy(tok_hbm, tokens_at(0), loc_sem.at[0])
    own_tokens.start()
    own_weights = [weight_copies(core, h, lambda src, dst, i: pltpu.make_async_copy(src, dst, loc_sem.at[2 + i])) for h in range(2)]
    own_down = pltpu.make_async_copy(down_hbm, wd, loc_sem.at[1])
    for copy in own_weights[0]:
        copy.start()

    barrier = pltpu.get_barrier_semaphore()
    peers = [sibling, first(1), first(2), first(3), second(1), second(2), second(3)] + [along_z(s) for s in (1, 7)]
    for peer in peers:
        pl.semaphore_signal(barrier, inc=1, device_id=peer, device_id_type=MESH)
    pl.semaphore_wait(barrier, len(peers))

    def swap_weights(h):
        return weight_copies(1 - core, h, lambda src, dst, i: go(remote(src, dst, w_ss.at[i], w_rs.at[i], sibling)))

    def pass_tokens(src, o, step):
        return go(remote(src, tokens_at(o), t_ss.at[o], t_rs.at[o], along_z(step)))

    def share_tokens(o):
        return go(remote(tokens_at(o), tokens_at(o), f_ss.at[o], f_rs.at[o], sibling))

    arrive = {1: pass_tokens(tok_hbm, 1, 7), 7: pass_tokens(tok_hbm, 7, 1)}
    swapped = [swap_weights(0)]
    for h in range(1, len(PIECES)):
        for copy in own_weights[h]:
            copy.start()
    own_down.start()
    own_tokens.wait()
    shared = {0: share_tokens(0)}

    def relay(distance):
        for o in (distance, 8 - distance)[:1 if distance == 4 else 2]:
            arrive[o].wait_recv()
            shared[o] = share_tokens(o)
            if o < 4:
                arrive[o + 1] = pass_tokens(tokens_at(o), o + 1, 7)
            elif o > 5:
                arrive[o - 1] = pass_tokens(tokens_at(o), o - 1, 1)

    def weights_ready(h):
        for copy in own_weights[h]:
            copy.wait()
        for copy in swapped[h]:
            copy.wait_recv()

    def span(h, width=2):
        return pl.ds(width * starts[h], width * PIECES[h])

    def over_tiles(h, body, unroll=False):
        @pl.loop(0, 2 * PIECES[h] // TILE, unroll=unroll)
        def _(n):
            body(pl.ds(pl.multiple_of(2 * starts[h] + n * TILE, TILE), TILE))

    s1, s2, g1, g2, sib = {}, {}, {}, {}, {}
    zs = {}

    def scatter(c, src, dst, landing, ss, rs, to):
        i = 2 * c[0] + c[1]
        for d in (2, 1, 3):
            remote(src(d), dst(d), ss.at[i], rs.at[i], to(d)).start()
        three = remote(landing, landing, ss.at[i], rs.at[i], to(1))
        sent.append(three)
        return three

    def stage_m(c):
        g, h = c
        if h == 0:
            for o in OWNERS[g]:
                shared[o].wait_recv()

        def body(at):
            acc = jnp.dot(tokc[g, 0], wb[0, :, at], preferred_element_type=jnp.float32)
            acc += jnp.dot(tokc[g, 1], wb[1, :, at], preferred_element_type=jnp.float32)
            pf[g, :, :, at] = acc.reshape(4, 32, TILE)
            pb[g, :, :, at] = acc.astype(jnp.bfloat16).reshape(4, 32, TILE)

        over_tiles(h, body, unroll=True)
        s1[c] = scatter(c, lambda d: pb.at[g, (p + d) % 4, :, span(h)], lambda d: r1.at[g, d - 1, :, span(h)], r1.at[g, :, :, span(h)], s1_ss, s1_rs, first)

    def stage_1(c):
        g, h = c
        s1[c].wait_recv()

        def body(at):
            acc = pf[g, p, :, at]
            for d in range(3):
                acc += r1[g, d, :, at].astype(jnp.float32)
            acc = acc.reshape(4, 8, TILE)
            s2f[g, :, :, at] = acc
            s2b[g, :, :, at] = acc.astype(jnp.bfloat16)

        over_tiles(h, body)
        s2[c] = scatter(c, lambda d: s2b.at[g, (q + d) % 4, :, span(h)], lambda d: r2.at[g, d - 1, :, span(h)], r2.at[g, :, :, span(h)], s2_ss, s2_rs, second)

    def stage_2(c):
        g, h = c
        s2[c].wait_recv()
        acc = s2f[g, q, :, span(h)]
        for d in range(3):
            acc += r2[g, d, :, span(h)].astype(jnp.float32)
        gate, up = acc[:, :PIECES[h]], acc[:, PIECES[h]:]
        hid[core, g, p * 4 + q, :, span(h, 1)] = (gate / (1.0 + jnp.exp(-gate)) * up).astype(jnp.bfloat16)
        place = hid.at[core, g, p * 4 + q, :, span(h, 1)]
        g1[c] = scatter(c, lambda d: place, lambda d: place, hid.at[core, g, pl.ds(0, 3), :, span(h, 1)], g1_ss, g1_rs, second)

    def stage_3(c):
        g, h = c
        g1[c].wait_recv()
        place = hid.at[core, g, pl.ds(p * 4, 4), :, span(h, 1)]
        g2[c] = scatter(c, lambda d: place, lambda d: place, hid.at[core, g, pl.ds(0, 12), :, span(h, 1)], g2_ss, g2_rs, first)

    def stage_4(c):
        g, h = c
        g2[c].wait_recv()
        place = hid.at[core, g, :, :, span(h, 1)]
        sib[c] = go(remote(place, place, sib_ss.at[2 * g + h], sib_rs.at[2 * g + h], sibling))

    def stage_5(c):
        g, h = c
        sib[c].wait_recv()
        if c == (0, 0):
            own_down.wait()
        last = h == len(PIECES) - 1
        for j in range(2):
            o = OWNERS[g][j]
            part = None if h == 0 else ya[g, j]
            for i in range(2):
                units = hid[i, g, pl.ds(8 * j, 8), :, span(h, 1)].astype(jnp.float32).reshape(rows, PIECES[h]).astype(jnp.bfloat16)
                term = jnp.dot(units, wd[pl.ds(i * half + starts[h], PIECES[h]), :], preferred_element_type=jnp.float32)
                part = term if part is None else part + term
            if not last or o == 0:
                ya[g, j] = part
            else:
                yb[o] = part.astype(jnp.bfloat16)
                zs[o] = go(remote(yb.at[o], zr.at[o], z_ss.at[o], z_rs.at[o], along_z(o)))

    chunks = [(g, h) for g in range(GROUPS) for h in range(len(PIECES))]
    stages = (stage_m, stage_1, stage_2, stage_3, stage_4, stage_5)
    relay(1)
    weights_ready(0)
    swapped.append(swap_weights(1))
    for t in range(len(chunks) + LAGS[-1]):
        for stage, lag in zip(stages, LAGS):
            if 0 <= t - lag < len(chunks):
                stage(chunks[t - lag])
        if t in RELAYS:
            relay(RELAYS[t])
        if t == 0:
            weights_ready(1)

    for copy in sent:
        copy.wait_send()
    total = ya[0, 0]
    for g in range(GROUPS):
        for o in OWNERS[g]:
            if o:
                zs[o].wait_recv()
                total += zr[o].astype(jnp.float32)
    out_ref[...] = total.astype(jnp.bfloat16)


def on_device(tokens, gate_weight, up_weight, down_weight):
    rows, depth = tokens.shape
    hidden = gate_weight.shape[1]
    half = hidden // 2
    bf16, f32 = jnp.bfloat16, jnp.float32
    dma = pltpu.SemaphoreType.DMA
    n = GROUPS
    m = 2 * n
    return pl.pallas_call(
        kernel,
        out_shape=jax.ShapeDtypeStruct((rows, down_weight.shape[1]), bf16),
        in_specs=[pl.BlockSpec(memory_space=pl.ANY)] * 4,
        out_specs=pl.BlockSpec(memory_space=pltpu.VMEM),
        scratch_shapes=[
            pltpu.VMEM((2, depth, hidden), bf16),
            pltpu.VMEM(down_weight.shape, bf16),
            pltpu.VMEM((n, 2, 2 * rows, depth), bf16),
            pltpu.VMEM((n, 4, 32, hidden), f32),
            pltpu.VMEM((n, 4, 32, hidden), bf16),
            pltpu.VMEM((n, 3, 32, hidden), bf16),
            pltpu.VMEM((n, 4, 8, hidden), f32),
            pltpu.VMEM((n, 4, 8, hidden), bf16),
            pltpu.VMEM((n, 3, 8, hidden), bf16),
            pltpu.VMEM((2, n, 16, 8, half), bf16),
            pltpu.VMEM((n, 2, rows, down_weight.shape[1]), f32),
            pltpu.VMEM((8, rows, down_weight.shape[1]), bf16),
            pltpu.VMEM((8, rows, down_weight.shape[1]), bf16),
            dma((6,)), dma((4,)), dma((4,)),
            dma((8,)), dma((8,)), dma((8,)), dma((8,)),
            dma((m,)), dma((m,)), dma((m,)), dma((m,)),
            dma((m,)), dma((m,)), dma((m,)), dma((m,)),
            dma((m,)), dma((m,)), dma((8,)), dma((8,)),
        ],
        compiler_params=pltpu.CompilerParams(collective_id=0, has_side_effects=True, vmem_limit_bytes=56 << 20),
    )(tokens, gate_weight, up_weight, down_weight)


def solution(mesh):
    return jax.shard_map(
        on_device,
        mesh=mesh,
        in_specs=(P("gy", "gx"), P("gx", "gy"), P("gx", "gy"), P("gy", "gx")),
        out_specs=P("gy", "gx"),
        check_vma=False,
    )
```
